32 devices in a mesh: gx: 8 (over z, x), gy: 4 (over y, core).
Axes of the slice: x: 2, y: 2, z: 4, core: 2. Of those that a mesh axis runs over, the one named last changes fastest.
Arguments:
- features: bfloat16 [32768, 512], P(('gx', 'gy')), may hold values from -6 to 6
- zorder_rank: int32 [32768], P(('gx', 'gy')), may hold values from 0 to 32767, as said below
- hilbert_rank: int32 [32768], P(('gx', 'gy')), may hold values from 0 to 32767, as said below
- attention_gain: float32 [2, 512], replicated, may hold values from 0.1 to 1.9
- attention_in: bfloat16 [2, 512, 1536], replicated, may hold values from -2 to 2
- attention_out: bfloat16 [2, 512, 512], replicated, may hold values from -0.25 to 0.25
- feedforward_gain: float32 [2, 512], replicated, may hold values from 0.1 to 1.9
- feedforward_up: bfloat16 [2, 512, 2048], replicated, may hold values from -0.25 to 0.25
- feedforward_down: bfloat16 [2, 2048, 512], replicated, may hold values from -0.125 to 0.125
Outputs:
- output_rows: bfloat16 [32768, 512], P(('gx', 'gy'))
The draws below stay inside these ranges and needn't reach their ends.
Inputs may be any that keep to these rules, and one draw needn't show every extreme that they name: `zorder_rank`: every value appears once. Device d (gx index times 4 plus gy index) owns the ranks d * 1024 to d * 1024 + 1023. Of one device's points at most 80 have ranks in one device's range, and some device sends exactly 80 into some range. `hilbert_rank`: every value appears once, with ranges owned as for zorder_rank. Of one device's points at most 80 have ranks in one device's range; of the points whose zorder_rank lies in one device's range, at most 80 have hilbert_rank in one device's range; both bounds are reached.
All inputs are finite; a program needn't handle non-finite values.
Results may differ from the reference program's by a relative error of at most 0.03.
The reference program's roundings to bfloat16 on the way count: a program that leaves them out, or rounds other values in their place, can miss the bound.
Values may be sent and summed in bfloat16 or wider, within the bound.
No kernel may reach another device: no remote copies, remote signals or barrier semaphores. Data moves between devices by JAX's collectives and lax.ppermute only.
A program may use at most 128 MiB of HBM per device.

```python
import jax
import jax.numpy as jnp
from jax import lax

C = 512
HEADS = 32
PATCH = 1024
HID = 2048
ROWS = 1024
TOTAL = 32768


def shuffled(sub_key):
    return jax.random.permutation(sub_key, ROWS).astype(jnp.int32)


def curve_ranks(key):
    peer_count = TOTAL // ROWS
    half_count = peer_count // 2
    key_list = jax.random.split(jax.random.fold_in(key, 29), 9)
    offset = jax.random.permutation(key_list[0], half_count).astype(jnp.int32) + half_count * jax.random.randint(key_list[1], (half_count,), 0, 2)
    extra_shift = jax.random.randint(key_list[2], (), 0, peer_count)
    relabel = jax.random.permutation(key_list[3], peer_count).astype(jnp.int32)
    inverse = jnp.zeros((peer_count,), jnp.int32).at[relabel].set(jnp.arange(peer_count, dtype=jnp.int32))
    base_size = 2 * ROWS // peer_count
    most_spread = ROWS // (2 * peer_count)
    spread = jax.random.randint(key_list[4], (half_count // 2,), 0, most_spread + 1).at[0].set(most_spread)
    group_sizes = jnp.concatenate([base_size + spread, base_size - spread])
    group_sizes = group_sizes[jax.random.permutation(key_list[5], half_count)]
    bounds = jnp.cumsum(group_sizes)
    within = jnp.arange(ROWS, dtype=jnp.int32)
    group_of = jnp.sum((within[:, None] >= bounds[None, :]).astype(jnp.int32), axis=1)
    step_of = offset[group_of]
    device_label = inverse[:, None]
    zorder_owner = relabel[(device_label + step_of[None, :]) % peer_count]
    hilbert_owner = relabel[(device_label + 2 * step_of[None, :] + extra_shift) % peer_count]
    shuffle = jax.vmap(shuffled)(jax.random.split(key_list[6], peer_count))
    zorder_slot = jax.vmap(shuffled)(jax.random.split(key_list[7], peer_count))
    hilbert_slot = jax.vmap(shuffled)(jax.random.split(key_list[8], peer_count))
    zorder_value = zorder_owner * ROWS + zorder_slot[zorder_owner, within[None, :]]
    hilbert_value = hilbert_owner * ROWS + hilbert_slot[hilbert_owner, within[None, :]]
    sources = jnp.arange(peer_count, dtype=jnp.int32)[:, None]
    zorder_rank = jnp.zeros((peer_count, ROWS), jnp.int32).at[sources, shuffle].set(zorder_value)
    hilbert_rank = jnp.zeros((peer_count, ROWS), jnp.int32).at[sources, shuffle].set(hilbert_value)
    return (zorder_rank.reshape(TOTAL).astype(jnp.int32), hilbert_rank.reshape(TOTAL).astype(jnp.int32))


def draw_zorder_rank(key, part):
    return curve_ranks(key)[0]


def draw_hilbert_rank(key, part):
    return curve_ranks(key)[1]


def draw_attention_in(key, part):
    key_list = jax.random.split(jax.random.fold_in(key, 11), 1)
    dense_part = jax.random.normal(key_list[0], (2, C, 3 * C), jnp.float32) * C ** (-0.5)
    return jnp.clip(dense_part, -2.0, 2.0).astype(jnp.bfloat16)


def levels(rng, shape, pieces, low, top_value):
    def one(position, blocks):
        steps = jax.random.uniform(jax.random.fold_in(jax.random.fold_in(rng, 6), position), (blocks,), jnp.float32, low / len(pieces), top_value / len(pieces))
        return jnp.repeat(jnp.exp(steps), shape[position] // blocks).reshape((-1,) + (1,) * (len(shape) - position - 1))

    gain = one(*pieces[0])
    for cut in pieces[1:]:
        gain = gain * one(*cut)
    return gain


def noise(key, dims, width, most, pieces=(), held_as=jnp.bfloat16):
    level = levels(key, dims, pieces, -0.22, 0.18) if pieces else 1.0
    values = jax.random.normal(key, dims, jnp.float32) * width * level
    return jnp.minimum(jnp.maximum(values, -most), most).astype(held_as)


def setup_inputs(seed: int = 0) -> dict:
    streams_of = jax.random.split(jax.random.key(seed), 10)
    return {
        "features": noise(streams_of[0], (TOTAL, C), 1.0, 6.0, ((0, 32),)),
        "zorder_rank": draw_zorder_rank(jax.random.fold_in(streams_of[9], 71), 0),
        "hilbert_rank": draw_hilbert_rank(jax.random.fold_in(streams_of[9], 71), 0),
        "attention_gain": jnp.clip(1.0 + 0.18 * jax.random.normal(streams_of[3], (2, C), jnp.float32), 0.1, 1.9),
        "attention_in": draw_attention_in(jax.random.fold_in(streams_of[9], 71), 0),
        "attention_out": noise(streams_of[5], (2, C, C), C ** -0.5, 0.25),
        "feedforward_gain": jnp.clip(1.0 + 0.18 * jax.random.normal(streams_of[6], (2, C), jnp.float32), 0.1, 1.9),
        "feedforward_up": noise(streams_of[7], (2, C, HID), C ** -0.5, 0.25),
        "feedforward_down": noise(streams_of[8], (2, HID, C), HID ** -0.5, 0.125),
    }


epsilon = 1e-05

def layer_norm(row_block, row_gain):
    values = row_block.astype(jnp.float32)
    average = lax.optimization_barrier(jnp.mean(values, axis=-1, keepdims=True))
    centred = values - average
    variance = lax.optimization_barrier(jnp.mean(centred * centred, axis=-1, keepdims=True))
    return (centred * lax.rsqrt(variance + epsilon) * row_gain).astype(jnp.bfloat16)

def patch_attention(projected):
    head_size = C // HEADS
    split_heads = projected.astype(jnp.float32).reshape(PATCH, 3, HEADS, head_size)
    scores = jnp.einsum('qhd,khd->hqk', split_heads[:, 0], split_heads[:, 1]) * head_size ** (-0.5)
    row_max = lax.optimization_barrier(jnp.max(scores, axis=2, keepdims=True))
    raised = jnp.exp(scores - row_max)
    weights = (raised / lax.optimization_barrier(jnp.sum(raised, axis=2, keepdims=True))).astype(jnp.bfloat16)
    mixed_rows = jnp.einsum('hqk,khd->qhd', weights.astype(jnp.float32), split_heads[:, 2])
    return mixed_rows.reshape(PATCH, C).astype(jnp.bfloat16)

def transformer_block(stream, layer_index, attention_gain, attention_in, attention_out, feedforward_gain, feedforward_up, feedforward_down):
    normed = layer_norm(stream, attention_gain[layer_index])
    projected = jnp.dot(normed, attention_in[layer_index], preferred_element_type=jnp.float32).astype(jnp.bfloat16)
    mixed_rows = lax.map(patch_attention, projected.reshape(-1, PATCH, 3 * C)).reshape(-1, C)
    stream = (stream.astype(jnp.float32) + jnp.dot(mixed_rows, attention_out[layer_index], preferred_element_type=jnp.float32)).astype(jnp.bfloat16)
    normed = layer_norm(stream, feedforward_gain[layer_index])
    hidden = jax.nn.gelu(jnp.dot(normed, feedforward_up[layer_index], preferred_element_type=jnp.float32), approximate=False).astype(jnp.bfloat16)
    return (stream.astype(jnp.float32) + jnp.dot(hidden, feedforward_down[layer_index], preferred_element_type=jnp.float32)).astype(jnp.bfloat16)

def reference(features, zorder_rank, hilbert_rank, attention_gain, attention_in, attention_out, feedforward_gain, feedforward_up, feedforward_down):
    weights = (attention_gain, attention_in, attention_out, feedforward_gain, feedforward_up, feedforward_down)
    ordered = jnp.zeros_like(features).at[zorder_rank].set(features)
    ordered = transformer_block(ordered, 0, *weights)
    stream = ordered[zorder_rank]
    ordered = jnp.zeros_like(stream).at[hilbert_rank].set(stream)
    ordered = transformer_block(ordered, 1, *weights)
    return ordered[hilbert_rank]
```

```python
import functools

import jax
import jax.numpy as jnp
from jax import lax
from jax.experimental import pallas as pl
from jax.experimental.pallas import tpu as pltpu
from jax.sharding import PartitionSpec as P

HEADS = 32
PATCH = 1024
EPSILON = 1e-05
LOG2E = 1.4426950408889634
AXES = ("gx", "gy")
SAFE_EXPONENT = 80.0

bf16 = jnp.bfloat16
f32 = jnp.float32
i32 = jnp.int32


def call(kernel, name, out_shape, scratch=(), flops=0):
    def run(*args):
        vmem = pl.BlockSpec(memory_space=pltpu.VMEM)
        outs = jax.tree.map(lambda _: vmem, out_shape)
        moved = sum(a.size * a.dtype.itemsize for a in args)
        return pl.pallas_call(
            kernel,
            name=name,
            out_shape=out_shape,
            in_specs=[vmem] * len(args),
            out_specs=outs,
            scratch_shapes=scratch,
            compiler_params=pltpu.CompilerParams(vmem_limit_bytes=56 << 20),
            cost_estimate=pl.CostEstimate(flops=flops, bytes_accessed=moved, transcendentals=0),
        )(*args)

    return run


def column(row):
    return jnp.broadcast_to(row, (128, row.shape[1])).T


def order_in_bucket(keys, size):
    shift = size.bit_length() - 1
    tall = column(keys)
    pieces = []
    for start in range(0, keys.shape[1], 128):
        piece = keys[:, start : start + 128]
        low = lax.shift_left(lax.shift_right_logical(piece, shift), shift)
        inside = jnp.logical_and(tall >= low, tall < piece)
        pieces.append(jnp.sum(jnp.where(inside, 1.0, 0.0), axis=0, keepdims=True))
    return jnp.concatenate(pieces, axis=1).astype(i32)


def digits(*values):
    rows = []
    for value, count in values:
        for place in range(count):
            rows.append(
                jnp.bitwise_and(lax.shift_right_logical(value, 8 * place), 255).astype(f32)
            )
    rows += [jnp.zeros_like(rows[0])] * (8 - len(rows))
    return jnp.concatenate(rows, axis=0).astype(bf16)


def undigits(rows, start, count):
    value = rows[start : start + 1].astype(i32)
    for place in range(1, count):
        value = value + lax.shift_left(rows[start + place : start + place + 1].astype(i32), 8 * place)
    return value


def chosen(wanted, axis, start, rows, columns):
    index = lax.broadcasted_iota(i32, (rows, columns), axis) + start
    return jnp.where(wanted == index, 1.0, 0.0).astype(bf16)


def contract_last(a, b):
    return lax.dot_general(a, b, (((1,), (1,)), ((), ())), preferred_element_type=f32)


def send_tags_kernel(size, capacity, zr_ref, hr_ref, z_tag_ref, h_tag_ref, target_ref, home_ref):
    shift = size.bit_length() - 1
    zr, hr = zr_ref[...], hr_ref[...]
    row = lax.broadcasted_iota(i32, (1, size), 1)
    z_owner = lax.shift_right_logical(zr, shift)
    h_owner = lax.shift_right_logical(hr, shift)
    target = z_owner * capacity + order_in_bucket(z_owner * size + row, size)
    home = h_owner * capacity + order_in_bucket(hr, size)
    target_ref[...] = target
    home_ref[...] = home
    ones = jnp.ones_like(zr)
    for wanted, near, far, tag_ref in ((target, zr, hr, z_tag_ref), (home, hr, zr, h_tag_ref)):
        parts = digits((jnp.bitwise_and(near, size - 1), 2), (far, 3), (ones, 1))
        slots = tag_ref.shape[1]
        for start in range(0, slots, 512):
            picked = contract_last(parts, chosen(wanted, 0, start, 512, size))
            near_value = undigits(picked, 0, 2)
            far_value = undigits(picked, 2, 3)
            there = picked[5:6] > 0.5
            tag_ref[:, start : start + 512] = jnp.where(there, far_value * size + near_value, -1)


def route_kernel(size, capacity, z_tag_ref, h_tag_ref, place_ref, target2_ref, source2_ref, target3_ref):
    shift = size.bit_length() - 1
    slots = z_tag_ref.shape[1]
    z_tag, h_tag = z_tag_ref[...], h_tag_ref[...]
    z_place = jnp.where(z_tag < 0, -1, jnp.bitwise_and(z_tag, size - 1))
    h_place = jnp.where(h_tag < 0, -1, jnp.bitwise_and(h_tag, size - 1))
    place_ref[...] = z_place
    slot = lax.broadcasted_iota(i32, (1, slots), 1)
    peer = jnp.zeros((1, slots), f32)
    peer = jnp.floor((slot.astype(f32) + 0.5) * (1.0 / capacity)).astype(i32)
    z_parts = digits((lax.shift_right_logical(jnp.maximum(z_tag, 0), shift), 3))
    h_parts = digits((lax.shift_right_logical(jnp.maximum(h_tag, 0), shift), 3), (peer, 1))
    z_pieces, h_pieces = [], []
    for start in range(0, size, 256):
        z_pieces.append(contract_last(z_parts, chosen(z_place, 0, start, 256, slots)))
        h_pieces.append(contract_last(h_parts, chosen(h_place, 0, start, 256, slots)))
    z_rows = jnp.concatenate(z_pieces, axis=1)
    h_rows = jnp.concatenate(h_pieces, axis=1)
    row = lax.broadcasted_iota(i32, (1, size), 1)
    owner = lax.shift_right_logical(undigits(z_rows, 0, 3), shift)
    target2_ref[...] = owner * capacity + order_in_bucket(owner * size + row, size)
    zr = undigits(h_rows, 0, 3)
    source2_ref[...] = lax.shift_right_logical(zr, shift) * capacity + order_in_bucket(zr, size)
    home = undigits(h_rows, 3, 1)
    target3_ref[...] = home * capacity + order_in_bucket(home * size + row, size)


def pack_rows(target, rows, out_ref):
    slots = out_ref.shape[0]

    def step(i, carry):
        start = pl.multiple_of(i * 256, 256)
        pick = chosen(target, 0, start, 256, rows.shape[0])
        out_ref[pl.ds(start, 256), :] = jnp.dot(
            pick, rows, preferred_element_type=f32
        ).astype(bf16)
        return carry

    lax.fori_loop(0, slots // 256, step, 0, unroll=2)


def pack_kernel(target_ref, rows_ref, out_ref):
    pack_rows(target_ref[...], rows_ref[...], out_ref)


def unpack_kernel(source_ref, received_ref, out_ref, tall_ref):
    slots = received_ref.shape[0]
    tall_ref[...] = column(source_ref[...])

    def step(i, carry):
        start = pl.multiple_of(i * 256, 256)
        tall = tall_ref[pl.ds(start, 256), :]
        pick = jnp.concatenate(
            [chosen(tall, 1, piece, 256, 128) for piece in range(0, slots, 128)], axis=1
        )
        out_ref[pl.ds(start, 256), :] = jnp.dot(
            pick, received_ref[...], preferred_element_type=f32
        ).astype(bf16)
        return carry

    lax.fori_loop(0, out_ref.shape[0] // 256, step, 0, unroll=2)


def normalize(values, gain):
    values = values.astype(f32)
    centred = values - jnp.mean(values, axis=-1, keepdims=True)
    variance = jnp.mean(centred * centred, axis=-1, keepdims=True)
    return (centred * lax.rsqrt(variance + EPSILON) * gain).astype(bf16)


def project_kernel(
    by_source, heads, index_ref, received_ref, gain_ref, weight_ref,
    rows_ref, q_ref, k_ref, vt_ref, bound_ref, tall_ref,
):
    slots, width = received_ref.shape
    head_size = width // heads
    scale = head_size ** (-0.5) * LOG2E
    if by_source:
        tall_ref[...] = column(index_ref[...])
    group = jnp.where(
        lax.broadcasted_iota(i32, (width, 128), 0) // head_size
        == lax.broadcasted_iota(i32, (width, 128), 1),
        1.0,
        0.0,
    ).astype(bf16)
    block = 256

    def step(i, carry):
        q_most, k_most = carry
        start = pl.multiple_of(i * block, block)
        if by_source:
            tall = tall_ref[pl.ds(start, block), :]
            pick = jnp.concatenate(
                [chosen(tall, 1, piece, block, 128) for piece in range(0, slots, 128)], axis=1
            )
        else:
            pick = chosen(index_ref[...], 0, start, block, slots)
        rows = jnp.dot(pick, received_ref[...], preferred_element_type=f32).astype(bf16)
        rows_ref[pl.ds(start, block), :] = rows
        normed = normalize(rows, gain_ref[...])
        q = (
            jnp.dot(normed, weight_ref[:, :width], preferred_element_type=f32) * scale
        ).astype(bf16)
        k = jnp.dot(normed, weight_ref[:, width : 2 * width], preferred_element_type=f32).astype(bf16)
        v = jnp.dot(normed, weight_ref[:, 2 * width :], preferred_element_type=f32)
        q_ref[pl.ds(start, block), :] = q
        k_ref[pl.ds(start, block), :] = k
        vt_ref[:, pl.ds(start, block)] = v.T.astype(bf16)
        q_size = jnp.dot(q * q, group, preferred_element_type=f32)
        k_size = jnp.dot(k * k, group, preferred_element_type=f32)
        q_most = jnp.maximum(q_most, jnp.max(q_size, axis=0, keepdims=True))
        k_most = jnp.maximum(k_most, jnp.max(k_size, axis=0, keepdims=True))
        return q_most, k_most

    zero = jnp.zeros((1, 128), f32)
    q_most, k_most = lax.fori_loop(0, rows_ref.shape[0] // block, step, (zero, zero))
    bound_ref[...] = q_most * k_most


def attend_kernel(heads, q_ref, k_ref, vt_ref, bound_ref, out_ref):
    size, width = q_ref.shape
    head_size = width // heads
    per_group = 128 // head_size
    lane_head = lax.broadcasted_iota(i32, (1, 128), 1) // head_size
    none = jnp.zeros((), bf16)
    ones = jnp.ones((16, size), bf16)

    def operands(head):
        group = pl.multiple_of((head // per_group) * 128, 128)
        mine = lane_head == head % per_group
        keys = jnp.where(mine, k_ref[:, pl.ds(group, 128)], none)
        first = pl.multiple_of(head * head_size, head_size)
        values = jnp.concatenate([vt_ref[pl.ds(first, head_size), :], ones], axis=0)
        return group, first, keys, values

    def finish(first, start, count, values, weights):
        mixed = jnp.dot(values, weights, preferred_element_type=f32)
        out_ref[pl.ds(first, head_size), pl.ds(start, count)] = (
            mixed[:head_size] / mixed[head_size : head_size + 1]
        ).astype(bf16)

    together = 2

    def small_scores(i, carry):
        for part in range(together):
            group, first, keys, values = operands(i * together + part)
            scores = contract_last(keys, q_ref[:, pl.ds(group, 128)])
            finish(first, 0, size, values, jnp.exp2(scores).astype(bf16))
        return carry

    def any_scores(head, carry):
        group, first, keys, values = operands(head)

        def tile(t, inner):
            start = pl.multiple_of(t * 256, 256)
            scores = contract_last(keys, q_ref[pl.ds(start, 256), pl.ds(group, 128)])
            scores = scores - jnp.max(scores, axis=0, keepdims=True)
            finish(first, start, 256, values, jnp.exp2(scores).astype(bf16))
            return inner

        return lax.fori_loop(0, size // 256, tile, carry)

    small = jnp.max(bound_ref[...]) <= SAFE_EXPONENT * SAFE_EXPONENT

    @pl.when(small)
    def _():
        lax.fori_loop(0, heads // together, small_scores, 0)

    @pl.when(jnp.logical_not(small))
    def _():
        lax.fori_loop(0, heads, any_scores, 0)


def gelu(x):
    size = jnp.abs(x)
    t = 1.0 / (1.0 + (0.3275911 * 0.7071067811865476) * size)
    series = 0.5 * 1.061405429
    for coefficient in (-1.453152027, 1.421413741, -0.284496736, 0.254829592):
        series = series * t + 0.5 * coefficient
    tail = series * t * jnp.exp2((x * x) * (-0.5 * LOG2E))
    return jnp.maximum(x, 0.0) - size * tail


def feed_kernel(
    target_ref, rows_ref, mixed_ref, out_weight_ref, gain_ref, up_ref, down_ref, packed_ref, block_ref
):
    size, width = rows_ref.shape
    hidden = up_ref.shape[1]
    block = 256
    piece = 512

    def step(i, carry):
        start = pl.multiple_of(i * block, block)
        mixed = lax.dot_general(
            mixed_ref[:, pl.ds(start, block)],
            out_weight_ref[...],
            (((0,), (0,)), ((), ())),
            preferred_element_type=f32,
        )
        stream = (rows_ref[pl.ds(start, block), :].astype(f32) + mixed).astype(bf16)
        normed = normalize(stream, gain_ref[...])
        total = stream.astype(f32)
        for first in range(0, hidden, piece):
            up = jnp.dot(normed, up_ref[:, first : first + piece], preferred_element_type=f32)
            total = total + jnp.dot(
                gelu(up).astype(bf16), down_ref[first : first + piece, :], preferred_element_type=f32
            )
        block_ref[pl.ds(start, block), :] = total.astype(bf16)
        return carry

    lax.fori_loop(0, size // block, step, 0)
    pack_rows(target_ref[...], block_ref[...], packed_ref)


def exchange(packed, peers):
    slots, width = packed.shape
    received = lax.all_to_all(
        packed.reshape(peers, slots // peers, width), AXES, split_axis=0, concat_axis=0, tiled=True
    )
    return received.reshape(slots, width)


def body(
    features, zorder_rank, hilbert_rank, attention_gain, attention_in, attention_out,
    feedforward_gain, feedforward_up, feedforward_down,
):
    size, width = features.shape
    peers = lax.axis_size("gx") * lax.axis_size("gy")
    capacity = 5 * size // (2 * peers)
    slots = peers * capacity
    hidden = feedforward_up.shape[2]

    def shape(rows, columns, dtype):
        return jax.ShapeDtypeStruct((rows, columns), dtype)

    index = shape(1, size, i32)
    tags = shape(1, slots, i32)
    z_tags, h_tags, target1, source3 = call(
        functools.partial(send_tags_kernel, size, capacity), "send_tags", (tags, tags, index, index)
    )(zorder_rank.reshape(1, size), hilbert_rank.reshape(1, size))
    both = jnp.concatenate([z_tags.reshape(peers, 1, capacity), h_tags.reshape(peers, 1, capacity)], axis=2)
    both = lax.all_to_all(both, AXES, split_axis=0, concat_axis=0, tiled=True)
    z_tags = both[:, 0, :capacity].reshape(1, slots)
    h_tags = both[:, 0, capacity:].reshape(1, slots)
    select = 2 * slots * size * width
    packed = call(pack_kernel, "pack", shape(slots, width, bf16), flops=select)(target1, features)
    received = exchange(packed, peers)
    place1, target2, source2, target3 = call(
        functools.partial(route_kernel, size, capacity), "route", (tags, index, index, index)
    )(z_tags, h_tags)

    for layer, incoming, outgoing in ((0, place1, target2), (1, source2, target3)):
        half = shape(size, width, bf16)
        rows, q, k, vt, bound = call(
            functools.partial(project_kernel, layer == 1, HEADS),
            "project",
            (half, half, half, shape(width, size, bf16), shape(1, 128, f32)),
            scratch=[pltpu.VMEM((size, 128), i32)],
            flops=select + 6 * size * width * width,
        )(incoming, received, attention_gain[layer].reshape(1, width), attention_in[layer])
        mixed = call(
            functools.partial(attend_kernel, HEADS),
            "attend",
            shape(width, size, bf16),
            flops=16 * size * size * width,
        )(q, k, vt, bound)
        packed = call(
            feed_kernel,
            "feed",
            shape(slots, width, bf16),
            scratch=[pltpu.VMEM((size, width), bf16)],
            flops=select + 2 * size * width * (width + 2 * hidden),
        )(
            outgoing, rows, mixed, attention_out[layer], feedforward_gain[layer].reshape(1, width),
            feedforward_up[layer], feedforward_down[layer],
        )
        received = exchange(packed, peers)

    return call(
        unpack_kernel,
        "unpack",
        shape(size, width, bf16),
        scratch=[pltpu.VMEM((size, 128), i32)],
        flops=select,
    )(source3, received)


def solution(mesh):
    split = P(AXES, None)
    return jax.shard_map(
        body,
        mesh=mesh,
        in_specs=(split, P(AXES), P(AXES), P(), P(), P(), P(), P(), P()),
        out_specs=split,
        check_vma=False,
    )
```

```python
import functools

import jax
import jax.numpy as jnp
from jax import lax
from jax.experimental import pallas as pl
from jax.experimental.pallas import tpu as pltpu
from jax.sharding import PartitionSpec as P

HEADS = 32
PATCH = 1024
EPSILON = 1e-05
LOG2E = 1.4426950408889634
AXES = ("gx", "gy")
SAFE_EXPONENT = 80.0

bf16 = jnp.bfloat16
f32 = jnp.float32
i32 = jnp.int32


def call(kernel, name, out_shape, scratch=(), flops=0):
    def run(*args):
        vmem = pl.BlockSpec(memory_space=pltpu.VMEM)
        outs = jax.tree.map(lambda _: vmem, out_shape)
        moved = sum(a.size * a.dtype.itemsize for a in args)
        return pl.pallas_call(
            kernel,
            name=name,
            out_shape=out_shape,
            in_specs=[vmem] * len(args),
            out_specs=outs,
            scratch_shapes=scratch,
            compiler_params=pltpu.CompilerParams(vmem_limit_bytes=56 << 20),
            cost_estimate=pl.CostEstimate(flops=flops, bytes_accessed=moved, transcendentals=0),
        )(*args)

    return run


def column(row):
    return jnp.broadcast_to(row, (128, row.shape[1])).T


def order_in_bucket(keys, size):
    shift = size.bit_length() - 1
    tall = column(keys)
    pieces = []
    for start in range(0, keys.shape[1], 128):
        piece = keys[:, start : start + 128]
        low = lax.shift_left(lax.shift_right_logical(piece, shift), shift)
        inside = jnp.logical_and(tall >= low, tall < piece)
        pieces.append(jnp.sum(jnp.where(inside, 1.0, 0.0), axis=0, keepdims=True))
    return jnp.concatenate(pieces, axis=1).astype(i32)


def digits(*values):
    rows = []
    for value, count in values:
        for place in range(count):
            rows.append(
                jnp.bitwise_and(lax.shift_right_logical(value, 8 * place), 255).astype(f32)
            )
    rows += [jnp.zeros_like(rows[0])] * (8 - len(rows))
    return jnp.concatenate(rows, axis=0).astype(bf16)


def undigits(rows, start, count):
    value = rows[start : start + 1].astype(i32)
    for place in range(1, count):
        value = value + lax.shift_left(rows[start + place : start + place + 1].astype(i32), 8 * place)
    return value


def chosen(wanted, axis, start, rows, columns):
    index = lax.broadcasted_iota(i32, (rows, columns), axis) + start
    return jnp.where(wanted == index, 1.0, 0.0).astype(bf16)


def contract_last(a, b):
    return lax.dot_general(a, b, (((1,), (1,)), ((), ())), preferred_element_type=f32)


def send_tags_kernel(size, capacity, zr_ref, hr_ref, z_tag_ref, h_tag_ref, target_ref, home_ref):
    shift = size.bit_length() - 1
    zr, hr = zr_ref[...], hr_ref[...]
    row = lax.broadcasted_iota(i32, (1, size), 1)
    z_owner = lax.shift_right_logical(zr, shift)
    h_owner = lax.shift_right_logical(hr, shift)
    target = z_owner * capacity + order_in_bucket(z_owner * size + row, size)
    home = h_owner * capacity + order_in_bucket(hr, size)
    target_ref[...] = target
    home_ref[...] = home
    peers = z_tag_ref.shape[0]
    ones = jnp.ones_like(zr)
    peer = lax.broadcasted_iota(i32, (peers, 1), 0)
    lane = lax.broadcasted_iota(i32, (128, 1), 0)
    for owner, wanted, near, far, tag_ref in (
        (z_owner, target, zr, hr, z_tag_ref),
        (h_owner, home, hr, zr, h_tag_ref),
    ):
        place = wanted - owner * capacity
        parts = digits((jnp.bitwise_and(near, size - 1), 2), (far, 3), (ones, 1)).astype(f32)
        mine = jnp.where(owner == peer, 1.0, 0.0)
        spread = jnp.where(place == lane, 1.0, 0.0).astype(bf16)
        tall = jnp.concatenate([mine * parts[d : d + 1] for d in range(6)], axis=0).astype(bf16)
        found = contract_last(tall, spread).astype(i32)

        def value(first, count):
            total = found[first * peers : (first + 1) * peers]
            for d in range(1, count):
                low = (first + d) * peers
                total = total + lax.shift_left(found[low : low + peers], 8 * d)
            return total

        tag_ref[...] = jnp.where(value(5, 1) > 0, value(2, 3) * size + value(0, 2), -1)


def route_kernel(size, capacity, z_tag_ref, h_tag_ref, place_ref, target2_ref, source2_ref, target3_ref):
    shift = size.bit_length() - 1
    slots = z_tag_ref.shape[1]
    z_tag, h_tag = z_tag_ref[...], h_tag_ref[...]
    z_place = jnp.where(z_tag < 0, -1, jnp.bitwise_and(z_tag, size - 1))
    h_place = jnp.where(h_tag < 0, -1, jnp.bitwise_and(h_tag, size - 1))
    place_ref[...] = z_place
    slot = lax.broadcasted_iota(i32, (1, slots), 1)
    peer = jnp.zeros((1, slots), f32)
    peer = jnp.floor((slot.astype(f32) + 0.5) * (1.0 / capacity)).astype(i32)
    z_parts = digits((lax.shift_right_logical(jnp.maximum(z_tag, 0), shift), 3))
    h_parts = digits((lax.shift_right_logical(jnp.maximum(h_tag, 0), shift), 3), (peer, 1))
    z_pieces, h_pieces = [], []
    for start in range(0, size, 256):
        z_pieces.append(contract_last(z_parts, chosen(z_place, 0, start, 256, slots)))
        h_pieces.append(contract_last(h_parts, chosen(h_place, 0, start, 256, slots)))
    z_rows = jnp.concatenate(z_pieces, axis=1)
    h_rows = jnp.concatenate(h_pieces, axis=1)
    row = lax.broadcasted_iota(i32, (1, size), 1)
    owner = lax.shift_right_logical(undigits(z_rows, 0, 3), shift)
    target2_ref[...] = owner * capacity + order_in_bucket(owner * size + row, size)
    zr = undigits(h_rows, 0, 3)
    source2_ref[...] = lax.shift_right_logical(zr, shift) * capacity + order_in_bucket(zr, size)
    home = undigits(h_rows, 3, 1)
    target3_ref[...] = home * capacity + order_in_bucket(home * size + row, size)


def pack_rows(target, rows, out_ref):
    slots = out_ref.shape[0]

    def step(i, carry):
        start = pl.multiple_of(i * 256, 256)
        pick = chosen(target, 0, start, 256, rows.shape[0])
        out_ref[pl.ds(start, 256), :] = jnp.dot(
            pick, rows, preferred_element_type=f32
        ).astype(bf16)
        return carry

    lax.fori_loop(0, slots // 256, step, 0, unroll=2)


def pack_kernel(target_ref, rows_ref, out_ref):
    pack_rows(target_ref[...], rows_ref[...], out_ref)


def unpack_kernel(source_ref, received_ref, out_ref, tall_ref):
    slots = received_ref.shape[0]
    tall_ref[...] = column(source_ref[...])

    def step(i, carry):
        start = pl.multiple_of(i * 256, 256)
        tall = tall_ref[pl.ds(start, 256), :]
        pick = jnp.concatenate(
            [chosen(tall, 1, piece, 256, 128) for piece in range(0, slots, 128)], axis=1
        )
        out_ref[pl.ds(start, 256), :] = jnp.dot(
            pick, received_ref[...], preferred_element_type=f32
        ).astype(bf16)
        return carry

    lax.fori_loop(0, out_ref.shape[0] // 256, step, 0, unroll=2)


def normalize(values, gain):
    values = values.astype(f32)
    centred = values - jnp.mean(values, axis=-1, keepdims=True)
    variance = jnp.mean(centred * centred, axis=-1, keepdims=True)
    return (centred * lax.rsqrt(variance + EPSILON) * gain).astype(bf16)


def attend(heads, small, q_ref, k_ref, vt_ref, out_ref):
    size, width = q_ref.shape
    head_size = width // heads
    per_group = 128 // head_size
    lane_head = lax.broadcasted_iota(i32, (1, 128), 1) // head_size
    none = jnp.zeros((), bf16)
    ones = jnp.ones((16, size), bf16)

    def operands(head):
        group = pl.multiple_of((head // per_group) * 128, 128)
        mine = lane_head == head % per_group
        keys = jnp.where(mine, k_ref[:, pl.ds(group, 128)], none)
        first = pl.multiple_of(head * head_size, head_size)
        values = jnp.concatenate([vt_ref[pl.ds(first, head_size), :], ones], axis=0)
        return group, first, keys, values

    def finish(first, start, count, values, weights):
        mixed = jnp.dot(values, weights, preferred_element_type=f32)
        out_ref[pl.ds(first, head_size), pl.ds(start, count)] = (
            mixed[:head_size] / mixed[head_size : head_size + 1]
        ).astype(bf16)

    together = 2

    def small_scores(i, carry):
        for part in range(together):
            group, first, keys, values = operands(i * together + part)
            scores = contract_last(keys, q_ref[:, pl.ds(group, 128)])
            finish(first, 0, size, values, jnp.exp2(scores).astype(bf16))
        return carry

    def any_scores(head, carry):
        group, first, keys, values = operands(head)

        def tile(t, inner):
            start = pl.multiple_of(t * 256, 256)
            scores = contract_last(keys, q_ref[pl.ds(start, 256), pl.ds(group, 128)])
            scores = scores - jnp.max(scores, axis=0, keepdims=True)
            finish(first, start, 256, values, jnp.exp2(scores).astype(bf16))
            return inner

        return lax.fori_loop(0, size // 256, tile, carry)

    @pl.when(small)
    def _():
        lax.fori_loop(0, heads // together, small_scores, 0)

    @pl.when(jnp.logical_not(small))
    def _():
        lax.fori_loop(0, heads, any_scores, 0)


def gelu(x):
    return (0.5 * x) * (1.0 + lax.erf(x * 0.7071067811865476))


def block_kernel(
    layer, by_source, heads,
    index_ref, target_ref, gain_in_ref, gain_feed_ref,
    received_hbm, in_hbm, out_hbm, up_hbm, down_hbm,
    packed_hbm,
    received_ref, in_ref, out_ref, up_ref, down_ref, packed_ref,
    rows_ref, q_ref, k_ref, vt_ref, mixed_ref, block_ref, tall_ref, load_sem, store_sem,
):
    slots, width = received_ref.shape
    size = rows_ref.shape[0]
    hidden = up_ref.shape[1]
    head_size = width // heads
    scale = head_size ** (-0.5) * LOG2E
    loads = [
        pltpu.make_async_copy(source, target, load_sem.at[i])
        for i, (source, target) in enumerate(
            (
                (received_hbm, received_ref),
                (in_hbm.at[layer], in_ref),
                (out_hbm.at[layer], out_ref),
                (up_hbm.at[layer], up_ref),
                (down_hbm.at[layer], down_ref),
            )
        )
    ]
    for load in loads:
        load.start()
    if by_source:
        tall_ref[...] = column(index_ref[...])
    group = jnp.where(
        lax.broadcasted_iota(i32, (width, 128), 0) // head_size
        == lax.broadcasted_iota(i32, (width, 128), 1),
        1.0,
        0.0,
    ).astype(bf16)
    block = 256
    loads[0].wait()
    loads[1].wait()

    def project(i, carry):
        q_most, k_most = carry
        start = pl.multiple_of(i * block, block)
        if by_source:
            tall = tall_ref[pl.ds(start, block), :]
            pick = jnp.concatenate(
                [chosen(tall, 1, piece, block, 128) for piece in range(0, slots, 128)], axis=1
            )
        else:
            pick = chosen(index_ref[...], 0, start, block, slots)
        rows = jnp.dot(pick, received_ref[...], preferred_element_type=f32).astype(bf16)
        rows_ref[pl.ds(start, block), :] = rows
        normed = normalize(rows, gain_in_ref[...])
        q = (
            jnp.dot(normed, in_ref[:, :width], preferred_element_type=f32) * scale
        ).astype(bf16)
        k = jnp.dot(normed, in_ref[:, width : 2 * width], preferred_element_type=f32).astype(bf16)
        v = jnp.dot(normed, in_ref[:, 2 * width :], preferred_element_type=f32)
        q_ref[pl.ds(start, block), :] = q
        k_ref[pl.ds(start, block), :] = k
        vt_ref[:, pl.ds(start, block)] = v.T.astype(bf16)
        q_size = jnp.dot(q * q, group, preferred_element_type=f32)
        k_size = jnp.dot(k * k, group, preferred_element_type=f32)
        q_most = jnp.maximum(q_most, jnp.max(q_size, axis=0, keepdims=True))
        k_most = jnp.maximum(k_most, jnp.max(k_size, axis=0, keepdims=True))
        return q_most, k_most

    zero = jnp.zeros((1, 128), f32)
    q_most, k_most = lax.fori_loop(0, size // block, project, (zero, zero), unroll=2)
    small = jnp.max(q_most * k_most) <= SAFE_EXPONENT * SAFE_EXPONENT
    attend(heads, small, q_ref, k_ref, vt_ref, mixed_ref)
    for load in loads[2:]:
        load.wait()
    piece = 512

    def feed(i, carry):
        start = pl.multiple_of(i * block, block)
        mixed = lax.dot_general(
            mixed_ref[:, pl.ds(start, block)],
            out_ref[...],
            (((0,), (0,)), ((), ())),
            preferred_element_type=f32,
        )
        stream = (rows_ref[pl.ds(start, block), :].astype(f32) + mixed).astype(bf16)
        normed = normalize(stream, gain_feed_ref[...])
        total = stream.astype(f32)
        for first in range(0, hidden, piece):
            up = jnp.dot(normed, up_ref[:, first : first + piece], preferred_element_type=f32)
            total = total + jnp.dot(
                gelu(up).astype(bf16), down_ref[first : first + piece, :], preferred_element_type=f32
            )
        block_ref[pl.ds(start, block), :] = total.astype(bf16)
        return carry

    lax.fori_loop(0, size // block, feed, 0, unroll=2)
    stores = []
    for i, start in enumerate(range(0, slots, 256)):
        pick = chosen(target_ref[...], 0, start, 256, size)
        packed_ref[start : start + 256, :] = jnp.dot(
            pick, block_ref[...], preferred_element_type=f32
        ).astype(bf16)
        stores.append(
            pltpu.make_async_copy(
                packed_ref.at[pl.ds(start, 256)], packed_hbm.at[pl.ds(start, 256)], store_sem.at[i]
            )
        )
        stores[-1].start()
    for store in stores:
        store.wait()


def run_block(layer, by_source, index, target, received, gains_in, w_in, w_out, gains_feed, up, down):
    slots, width = received.shape
    size = target.shape[1]
    hidden = up.shape[2]
    vmem = pl.BlockSpec(memory_space=pltpu.VMEM)
    hbm = pl.BlockSpec(memory_space=pl.ANY)
    half = pltpu.VMEM((size, width), bf16)
    flops = 4 * slots * size * width + size * width * (8 * width + 4 * hidden + 16 * size)
    return pl.pallas_call(
        functools.partial(block_kernel, layer, by_source, HEADS),
        name="block",
        out_shape=jax.ShapeDtypeStruct((slots, width), bf16),
        in_specs=[vmem] * 4 + [hbm] * 5,
        out_specs=hbm,
        scratch_shapes=[
            pltpu.VMEM((slots, width), bf16),
            pltpu.VMEM((width, 3 * width), bf16),
            pltpu.VMEM((width, width), bf16),
            pltpu.VMEM((width, hidden), bf16),
            pltpu.VMEM((hidden, width), bf16),
            pltpu.VMEM((slots, width), bf16),
            half,
            half,
            half,
            pltpu.VMEM((width, size), bf16),
            pltpu.VMEM((width, size), bf16),
            half,
            pltpu.VMEM((size, 128), i32),
            pltpu.SemaphoreType.DMA((5,)),
            pltpu.SemaphoreType.DMA((slots // 256,)),
        ],
        compiler_params=pltpu.CompilerParams(vmem_limit_bytes=56 << 20),
        cost_estimate=pl.CostEstimate(
            flops=flops, bytes_accessed=4 * slots * width, transcendentals=0
        ),
    )(
        index, target, gains_in[layer].reshape(1, width), gains_feed[layer].reshape(1, width),
        received, w_in, w_out, up, down,
    )


def exchange(packed, peers):
    slots, width = packed.shape
    received = lax.all_to_all(
        packed.reshape(peers, slots // peers, width), AXES, split_axis=0, concat_axis=0, tiled=True
    )
    return received.reshape(slots, width)


def body(
    features, zorder_rank, hilbert_rank, attention_gain, attention_in, attention_out,
    feedforward_gain, feedforward_up, feedforward_down,
):
    size, width = features.shape
    peers = lax.axis_size("gx") * lax.axis_size("gy")
    capacity = 5 * size // (2 * peers)
    slots = peers * capacity

    def shape(rows, columns, dtype):
        return jax.ShapeDtypeStruct((rows, columns), dtype)

    index = shape(1, size, i32)
    tags = shape(1, slots, i32)
    sent = shape(peers, 128, i32)
    z_tags, h_tags, target1, source3 = call(
        functools.partial(send_tags_kernel, size, capacity), "send_tags", (sent, sent, index, index)
    )(zorder_rank.reshape(1, size), hilbert_rank.reshape(1, size))
    both = jnp.concatenate([z_tags, h_tags], axis=1).reshape(peers, 1, 256)
    both = lax.all_to_all(both, AXES, split_axis=0, concat_axis=0, tiled=True)
    z_tags = both[:, 0, :capacity].reshape(1, slots)
    h_tags = both[:, 0, 128 : 128 + capacity].reshape(1, slots)
    select = 2 * slots * size * width
    packed = call(pack_kernel, "pack", shape(slots, width, bf16), flops=select)(target1, features)
    received = exchange(packed, peers)
    place1, target2, source2, target3 = call(
        functools.partial(route_kernel, size, capacity), "route", (tags, index, index, index)
    )(z_tags, h_tags)

    for layer, incoming, outgoing in ((0, place1, target2), (1, source2, target3)):
        packed = run_block(
            layer, layer == 1, incoming, outgoing, received, attention_gain, attention_in,
            attention_out, feedforward_gain, feedforward_up, feedforward_down,
        )
        received = exchange(packed, peers)

    return call(
        unpack_kernel,
        "unpack",
        shape(size, width, bf16),
        scratch=[pltpu.VMEM((size, 128), i32)],
        flops=select,
    )(source3, received)


def solution(mesh):
    split = P(AXES, None)
    return jax.shard_map(
        body,
        mesh=mesh,
        in_specs=(split, P(AXES), P(AXES), P(), P(), P(), P(), P(), P()),
        out_specs=split,
        check_vma=False,
    )
```

```python
import functools

import jax
import jax.numpy as jnp
from jax import lax
from jax.experimental import pallas as pl
from jax.experimental.pallas import tpu as pltpu
from jax.sharding import PartitionSpec as P

HEADS = 32
PATCH = 1024
EPSILON = 1e-05
LOG2E = 1.4426950408889634
AXES = ("gx", "gy")
SAFE_EXPONENT = 80.0

bf16 = jnp.bfloat16
f32 = jnp.float32
i32 = jnp.int32


def call(kernel, name, out_shape, scratch=(), flops=0):
    def run(*args):
        vmem = pl.BlockSpec(memory_space=pltpu.VMEM)
        outs = jax.tree.map(lambda _: vmem, out_shape)
        moved = sum(a.size * a.dtype.itemsize for a in args)
        return pl.pallas_call(
            kernel,
            name=name,
            out_shape=out_shape,
            in_specs=[vmem] * len(args),
            out_specs=outs,
            scratch_shapes=scratch,
            compiler_params=pltpu.CompilerParams(vmem_limit_bytes=56 << 20),
            cost_estimate=pl.CostEstimate(flops=flops, bytes_accessed=moved, transcendentals=0),
        )(*args)

    return run


def column(row):
    return jnp.broadcast_to(row, (128, row.shape[1])).T


def order_in_bucket(keys, size):
    shift = size.bit_length() - 1
    tall = column(keys)
    pieces = []
    for start in range(0, keys.shape[1], 128):
        piece = keys[:, start : start + 128]
        low = lax.shift_left(lax.shift_right_logical(piece, shift), shift)
        inside = jnp.logical_and(tall >= low, tall < piece)
        pieces.append(jnp.sum(jnp.where(inside, 1.0, 0.0), axis=0, keepdims=True))
    return jnp.concatenate(pieces, axis=1).astype(i32)


def digits(*values):
    rows = []
    for value, count in values:
        for place in range(count):
            rows.append(
                jnp.bitwise_and(lax.shift_right_logical(value, 8 * place), 255).astype(f32)
            )
    rows += [jnp.zeros_like(rows[0])] * (8 - len(rows))
    return jnp.concatenate(rows, axis=0).astype(bf16)


def undigits(rows, start, count):
    value = rows[start : start + 1].astype(i32)
    for place in range(1, count):
        value = value + lax.shift_left(rows[start + place : start + place + 1].astype(i32), 8 * place)
    return value


def chosen(wanted, axis, start, rows, columns):
    index = lax.broadcasted_iota(i32, (rows, columns), axis) + start
    return jnp.where(wanted == index, 1.0, 0.0).astype(bf16)


def contract_last(a, b):
    return lax.dot_general(a, b, (((1,), (1,)), ((), ())), preferred_element_type=f32)


def my_index():
    return lax.axis_index("gx") * lax.axis_size("gy") + lax.axis_index("gy")


def turned(index, peers):
    half = peers // 2
    return jnp.where(index >= half, 2 * (index - half) + 1, 2 * index)


def turned_back(index, peers):
    return index // 2 + (index % 2) * (peers // 2)


def send_tags_kernel(size, capacity, zr_ref, hr_ref, tag_ref, target_ref, source_ref):
    shift = size.bit_length() - 1
    peers = tag_ref.shape[0]
    zr, hr = zr_ref[...], hr_ref[...]
    row = lax.broadcasted_iota(i32, (1, size), 1)
    z_owner = lax.shift_right_logical(zr, shift)
    h_owner = lax.shift_right_logical(hr, shift)
    z_place = order_in_bucket(z_owner * size + row, size)
    h_place = order_in_bucket(hr, size)
    me = turned(my_index(), peers)
    target_ref[...] = jnp.bitwise_xor(turned(z_owner, peers), me) * capacity + z_place
    source_ref[...] = jnp.bitwise_xor(turned(h_owner, peers), me) * capacity + h_place
    ones = jnp.ones_like(zr)
    peer = lax.broadcasted_iota(i32, (peers, 1), 0)
    lane = lax.broadcasted_iota(i32, (128, 1), 0)
    for i, (owner, place, near, far) in enumerate(
        ((z_owner, z_place, zr, hr), (h_owner, h_place, hr, zr))
    ):
        parts = digits((jnp.bitwise_and(near, size - 1), 2), (far, 3), (ones, 1)).astype(f32)
        mine = jnp.where(owner == peer, 1.0, 0.0)
        spread = jnp.where(place == lane, 1.0, 0.0).astype(bf16)
        tall = jnp.concatenate([mine * parts[d : d + 1] for d in range(6)], axis=0).astype(bf16)
        found = contract_last(tall, spread).astype(i32)

        def value(first, count):
            total = found[first * peers : (first + 1) * peers]
            for d in range(1, count):
                low = (first + d) * peers
                total = total + lax.shift_left(found[low : low + peers], 8 * d)
            return total

        tag_ref[:, i * 128 : (i + 1) * 128] = jnp.where(
            value(5, 1) > 0, value(2, 3) * size + value(0, 2), -1
        )


def from_xor(table, me):
    peers = table.shape[0]
    row = lax.broadcasted_iota(i32, table.shape, 0)
    bit = 1
    while bit < peers:
        up = pltpu.roll(table, peers - bit, 0)
        down = pltpu.roll(table, bit, 0)
        swapped = jnp.where(jnp.bitwise_and(row, bit) == 0, up, down)
        table = jnp.where(jnp.bitwise_and(me, bit) == 0, table, swapped)
        bit *= 2
    return table


def offsets(counts):
    peers = counts.shape[0]
    row = lax.broadcasted_iota(i32, counts.shape, 0)
    total = counts
    step = 1
    while step < peers:
        total = total + jnp.where(row >= step, pltpu.roll(total, step, 0), 0)
        step *= 2
    return total - counts


def positions_of_slots(counts, first, capacity, slots):
    peers = counts.shape[0]
    owner = lax.broadcasted_iota(i32, (peers, 128), 0)
    pieces = []
    for start in range(0, slots, 128):
        slot = lax.broadcasted_iota(i32, (peers, 128), 1) + start
        place = slot - owner * capacity
        mine = jnp.logical_and(place >= 0, place < counts)
        pieces.append(jnp.sum(jnp.where(mine, first + place + 1, 0), axis=0, keepdims=True) - 1)
    return jnp.concatenate(pieces, axis=1)


def listed(tags, size):
    peers = tags.shape[0]
    counts = jnp.sum(jnp.where(tags >= 0, 1.0, 0.0), axis=1, keepdims=True).astype(i32)
    counts = jnp.broadcast_to(counts, (peers, 128))
    first = offsets(counts)
    position = lax.broadcasted_iota(i32, (1, size), 1)
    wide_first = jnp.concatenate([first] * (size // 128), axis=1)
    wide_end = jnp.concatenate([first + counts] * (size // 128), axis=1)
    within = jnp.logical_and(position >= wide_first, position < wide_end)
    mine = jnp.where(within, 1.0, 0.0)
    owner_index = lax.broadcasted_iota(i32, (peers, size), 0)
    owner = jnp.sum(jnp.where(within, owner_index, 0), axis=0, keepdims=True)
    place = position - jnp.sum(jnp.where(within, wide_first, 0), axis=0, keepdims=True)
    at_place = lax.broadcasted_iota(i32, (128, size), 0) == place
    shift = size.bit_length() - 1
    clean = jnp.maximum(tags, 0)
    near, far = jnp.bitwise_and(clean, size - 1), lax.shift_right_logical(clean, shift)
    mine = mine.astype(bf16)

    def fetch(values, count):
        total = jnp.zeros((1, size), i32)
        for d in range(count):
            digit = jnp.bitwise_and(lax.shift_right_logical(values, 8 * d), 255)
            spread = lax.dot_general(
                digit.astype(f32).astype(bf16), mine, (((0,), (0,)), ((), ())),
                preferred_element_type=f32,
            )
            picked = jnp.sum(jnp.where(at_place, spread, 0.0), axis=0, keepdims=True)
            total = total + lax.shift_left(picked.astype(i32), 8 * d)
        return total

    return owner, fetch(near, 2), fetch(far, 3), counts, first


def route_kernel(
    size, capacity, tag_ref, place1_ref, target2_ref, place2_ref, target3_ref
):
    shift = size.bit_length() - 1
    slots = place1_ref.shape[1]
    peers = tag_ref.shape[0]
    me = turned(my_index(), peers)
    tags = from_xor(tag_ref[...], me)
    owner, zs, hr, counts, first = listed(tags[:, :128], size)
    place1_ref[...] = positions_of_slots(counts, first, capacity, slots)
    goal = jnp.bitwise_xor(turned(lax.shift_right_logical(hr, shift), peers), me)
    target2_ref[...] = goal * capacity + order_in_bucket(goal * size + zs, size)
    home, hs, zr, counts, first = listed(tags[:, 128:], size)
    came = jnp.bitwise_xor(turned(lax.shift_right_logical(zr, shift), peers), me)
    position = order_in_bucket(came * size + jnp.bitwise_and(zr, size - 1), size * peers)
    came_from = came == lax.broadcasted_iota(i32, (peers, size), 0)
    counts = jnp.sum(jnp.where(came_from, 1.0, 0.0), axis=1, keepdims=True).astype(i32)
    counts = jnp.broadcast_to(counts, (peers, 128))
    place2_ref[...] = positions_of_slots(counts, offsets(counts), capacity, slots)
    target = home * capacity + order_in_bucket(home * size + hs, size)
    parts = digits((target, 2))
    for start in range(0, size, 256):
        picked = contract_last(parts, chosen(position, 0, start, 256, size))
        target3_ref[:, start : start + 256] = undigits(picked, 0, 2)


def pack_rows(target_ref, rows_ref, packed_ref, part_refs, sem):
    slots = packed_ref.shape[0]
    capacity = slots // len(part_refs)
    blocks = slots // 256

    def step(i, carry):
        start = pl.multiple_of(i * 256, 256)
        pick = chosen(target_ref[...], 0, start, 256, rows_ref.shape[0])
        packed_ref[pl.ds(start, 256), :] = jnp.dot(
            pick, rows_ref[...], preferred_element_type=f32
        ).astype(bf16)
        return carry

    copies = []
    done = 0
    for end in (blocks // 2, blocks):
        lax.fori_loop(done, end, step, 0)
        done = end
        while (len(copies) + 1) * capacity <= end * 256 and len(copies) < len(part_refs):
            i = len(copies)
            copies.append(
                pltpu.make_async_copy(
                    packed_ref.at[pl.ds(i * capacity, capacity)], part_refs[i], sem.at[i]
                )
            )
            copies[-1].start()
    for copy in copies:
        copy.wait()


def pack_kernel(target_ref, rows_ref, *rest):
    *part_refs, packed_ref, sem = rest
    pack_rows(target_ref, rows_ref, packed_ref, part_refs, sem)


def load_parts(part_refs, received_ref, sem):
    capacity = received_ref.shape[0] // len(part_refs)
    copies = [
        pltpu.make_async_copy(part, received_ref.at[pl.ds(i * capacity, capacity)], sem.at[i])
        for i, part in enumerate(part_refs)
    ]
    for copy in copies:
        copy.start()
    return copies


def unpack_kernel(source_ref, *rest):
    *part_refs, out_ref, received_ref, tall_ref, sem = rest
    copies = load_parts(part_refs, received_ref, sem)
    slots = received_ref.shape[0]
    tall_ref[...] = column(source_ref[...])
    for copy in copies:
        copy.wait()

    def step(i, carry):
        start = pl.multiple_of(i * 256, 256)
        tall = tall_ref[pl.ds(start, 256), :]
        pick = jnp.concatenate(
            [chosen(tall, 1, piece, 256, 128) for piece in range(0, slots, 128)], axis=1
        )
        out_ref[pl.ds(start, 256), :] = jnp.dot(
            pick, received_ref[...], preferred_element_type=f32
        ).astype(bf16)
        return carry

    lax.fori_loop(0, out_ref.shape[0] // 256, step, 0, unroll=2)


def normalize(values, gain):
    values = values.astype(f32)
    centred = values - jnp.mean(values, axis=-1, keepdims=True)
    variance = jnp.mean(centred * centred, axis=-1, keepdims=True)
    return (centred * lax.rsqrt(variance + EPSILON) * gain).astype(bf16)


def attend(heads, small, q_ref, k_ref, vt_ref, out_ref):
    size, width = q_ref.shape
    head_size = width // heads
    per_group = 128 // head_size
    lane_head = lax.broadcasted_iota(i32, (1, 128), 1) // head_size
    none = jnp.zeros((), bf16)
    ones = jnp.ones((16, size), bf16)

    def operands(head):
        group = pl.multiple_of((head // per_group) * 128, 128)
        mine = lane_head == head % per_group
        keys = jnp.where(mine, k_ref[:, pl.ds(group, 128)], none)
        first = pl.multiple_of(head * head_size, head_size)
        values = jnp.concatenate([vt_ref[pl.ds(first, head_size), :], ones], axis=0)
        return group, first, keys, values

    def finish(first, start, count, values, weights):
        mixed = jnp.dot(values, weights, preferred_element_type=f32)
        out_ref[pl.ds(first, head_size), pl.ds(start, count)] = (
            mixed[:head_size] / mixed[head_size : head_size + 1]
        ).astype(bf16)

    together = 2

    def small_scores(i, carry):
        for part in range(together):
            group, first, keys, values = operands(i * together + part)
            scores = contract_last(keys, q_ref[:, pl.ds(group, 128)])
            finish(first, 0, size, values, jnp.exp2(scores).astype(bf16))
        return carry

    def any_scores(head, carry):
        group, first, keys, values = operands(head)

        def tile(t, inner):
            start = pl.multiple_of(t * 256, 256)
            scores = contract_last(keys, q_ref[pl.ds(start, 256), pl.ds(group, 128)])
            scores = scores - jnp.max(scores, axis=0, keepdims=True)
            finish(first, start, 256, values, jnp.exp2(scores).astype(bf16))
            return inner

        return lax.fori_loop(0, size // 256, tile, carry)

    @pl.when(small)
    def _():
        lax.fori_loop(0, heads // together, small_scores, 0)

    @pl.when(jnp.logical_not(small))
    def _():
        lax.fori_loop(0, heads, any_scores, 0)


def gelu(x):
    return (0.5 * x) * (1.0 + lax.erf(x * 0.7071067811865476))


def block_kernel(layer, heads, peers, *refs):
    place_ref, target_ref, gain_in_ref, gain_feed_ref, in_hbm, out_hbm, up_hbm, down_hbm = refs[:8]
    part_refs, packed_refs = refs[8 : 8 + peers], refs[8 + peers : 8 + 2 * peers]
    (
        received_ref, in_ref, out_ref, up_ref, down_ref, packed_ref,
        rows_ref, q_ref, k_ref, vt_ref, mixed_ref, block_ref, load_sem, part_sem, store_sem,
    ) = refs[8 + 2 * peers :]
    slots, width = received_ref.shape
    size = rows_ref.shape[0]
    hidden = up_ref.shape[1]
    head_size = width // heads
    scale = head_size ** (-0.5) * LOG2E
    arrivals = load_parts(part_refs, received_ref, part_sem)
    loads = [
        pltpu.make_async_copy(source.at[layer], target, load_sem.at[i])
        for i, (source, target) in enumerate(
            ((in_hbm, in_ref), (out_hbm, out_ref), (up_hbm, up_ref), (down_hbm, down_ref))
        )
    ]
    for load in loads:
        load.start()
    group = jnp.where(
        lax.broadcasted_iota(i32, (width, 128), 0) // head_size
        == lax.broadcasted_iota(i32, (width, 128), 1),
        1.0,
        0.0,
    ).astype(bf16)
    block = 256
    for arrival in arrivals:
        arrival.wait()
    loads[0].wait()

    def project(i, carry):
        q_most, k_most = carry
        start = pl.multiple_of(i * block, block)
        pick = chosen(place_ref[...], 0, start, block, slots)
        rows = jnp.dot(pick, received_ref[...], preferred_element_type=f32).astype(bf16)
        rows_ref[pl.ds(start, block), :] = rows
        normed = normalize(rows, gain_in_ref[...])
        q = (
            jnp.dot(normed, in_ref[:, :width], preferred_element_type=f32) * scale
        ).astype(bf16)
        k = jnp.dot(normed, in_ref[:, width : 2 * width], preferred_element_type=f32).astype(bf16)
        v = jnp.dot(normed, in_ref[:, 2 * width :], preferred_element_type=f32)
        q_ref[pl.ds(start, block), :] = q
        k_ref[pl.ds(start, block), :] = k
        vt_ref[:, pl.ds(start, block)] = v.T.astype(bf16)
        q_size = jnp.dot(q * q, group, preferred_element_type=f32)
        k_size = jnp.dot(k * k, group, preferred_element_type=f32)
        q_most = jnp.maximum(q_most, jnp.max(q_size, axis=0, keepdims=True))
        k_most = jnp.maximum(k_most, jnp.max(k_size, axis=0, keepdims=True))
        return q_most, k_most

    zero = jnp.zeros((1, 128), f32)
    q_most, k_most = lax.fori_loop(0, size // block, project, (zero, zero), unroll=2)
    small = jnp.max(q_most * k_most) <= SAFE_EXPONENT * SAFE_EXPONENT
    attend(heads, small, q_ref, k_ref, vt_ref, mixed_ref)
    for load in loads[1:]:
        load.wait()
    piece = 512

    def feed(i, carry):
        start = pl.multiple_of(i * block, block)
        mixed = lax.dot_general(
            mixed_ref[:, pl.ds(start, block)],
            out_ref[...],
            (((0,), (0,)), ((), ())),
            preferred_element_type=f32,
        )
        stream = (rows_ref[pl.ds(start, block), :].astype(f32) + mixed).astype(bf16)
        normed = normalize(stream, gain_feed_ref[...])
        total = stream.astype(f32)
        for first in range(0, hidden, piece):
            up = jnp.dot(normed, up_ref[:, first : first + piece], preferred_element_type=f32)
            total = total + jnp.dot(
                gelu(up).astype(bf16), down_ref[first : first + piece, :], preferred_element_type=f32
            )
        block_ref[pl.ds(start, block), :] = total.astype(bf16)
        return carry

    lax.fori_loop(0, size // block, feed, 0, unroll=2)
    pack_rows(target_ref, block_ref, packed_ref, packed_refs, store_sem)


def parts_shape(slots, count, width):
    return [jax.ShapeDtypeStruct((slots // count, width), bf16)] * count


def run_block(layer, place, target, parts, gains_in, w_in, w_out, gains_feed, up, down):
    count = len(parts)
    width = parts[0].shape[1]
    slots = count * parts[0].shape[0]
    size = target.shape[1]
    hidden = up.shape[2]
    vmem = pl.BlockSpec(memory_space=pltpu.VMEM)
    hbm = pl.BlockSpec(memory_space=pl.ANY)
    half = pltpu.VMEM((size, width), bf16)
    flipped = pltpu.VMEM((width, size), bf16)
    flops = 4 * slots * size * width + size * width * (8 * width + 4 * hidden + 16 * size)
    return pl.pallas_call(
        functools.partial(block_kernel, layer, HEADS, count),
        name="block",
        out_shape=parts_shape(slots, count, width),
        in_specs=[vmem] * 4 + [hbm] * (4 + count),
        out_specs=[hbm] * count,
        scratch_shapes=[
            pltpu.VMEM((slots, width), bf16),
            pltpu.VMEM((width, 3 * width), bf16),
            pltpu.VMEM((width, width), bf16),
            pltpu.VMEM((width, hidden), bf16),
            pltpu.VMEM((hidden, width), bf16),
            pltpu.VMEM((slots, width), bf16),
            half,
            half,
            half,
            flipped,
            flipped,
            half,
            pltpu.SemaphoreType.DMA((4,)),
            pltpu.SemaphoreType.DMA((count,)),
            pltpu.SemaphoreType.DMA((count,)),
        ],
        compiler_params=pltpu.CompilerParams(vmem_limit_bytes=48 << 20),
        cost_estimate=pl.CostEstimate(
            flops=flops, bytes_accessed=4 * slots * width, transcendentals=0
        ),
    )(
        place, target, gains_in[layer].reshape(1, width), gains_feed[layer].reshape(1, width),
        w_in, w_out, up, down, *parts,
    )


def exchange(parts, peers):
    if len(parts) == peers:
        out = []
        for t, part in enumerate(parts):
            step = turned_back(t, peers)
            out.append(
                lax.ppermute(part, AXES, [(d, d ^ step) for d in range(peers)]) if t else part
            )
        return out
    (part,) = parts
    device = jnp.arange(peers, dtype=i32)
    me = my_index()
    stacked = part.reshape(peers, part.shape[0] // peers, part.shape[1])
    stacked = jnp.take(stacked, jnp.bitwise_xor(turned(device, peers), turned(me, peers)), axis=0)
    received = lax.all_to_all(stacked, AXES, split_axis=0, concat_axis=0, tiled=True)
    received = jnp.take(received, jnp.bitwise_xor(turned_back(device, peers), me), axis=0)
    return [received.reshape(part.shape)]


def body(
    features, zorder_rank, hilbert_rank, attention_gain, attention_in, attention_out,
    feedforward_gain, feedforward_up, feedforward_down,
):
    size, width = features.shape
    peers = lax.axis_size("gx") * lax.axis_size("gy")
    capacity = 5 * size // (2 * peers)
    slots = peers * capacity
    count = peers if peers <= 64 and capacity % 16 == 0 else 1

    def shape(rows, columns, dtype):
        return jax.ShapeDtypeStruct((rows, columns), dtype)

    index = shape(1, size, i32)
    places = shape(1, slots, i32)
    tags, target1, source3 = call(
        functools.partial(send_tags_kernel, size, capacity),
        "send_tags",
        (shape(peers, 256, i32), index, index),
    )(zorder_rank.reshape(1, size), hilbert_rank.reshape(1, size))
    tags = lax.all_to_all(
        tags.reshape(peers, 1, 256), AXES, split_axis=0, concat_axis=0, tiled=True
    )
    tags = tags.reshape(2, peers // 2, 256).transpose(1, 0, 2).reshape(peers, 256)
    select = 2 * slots * size * width
    vmem = pl.BlockSpec(memory_space=pltpu.VMEM)
    hbm = pl.BlockSpec(memory_space=pl.ANY)
    packed = pl.pallas_call(
        pack_kernel,
        name="pack",
        out_shape=parts_shape(slots, count, width),
        in_specs=[vmem, vmem],
        out_specs=[hbm] * count,
        scratch_shapes=[pltpu.VMEM((slots, width), bf16), pltpu.SemaphoreType.DMA((count,))],
        compiler_params=pltpu.CompilerParams(vmem_limit_bytes=32 << 20),
        cost_estimate=pl.CostEstimate(flops=select, bytes_accessed=0, transcendentals=0),
    )(target1, features)
    received = exchange(packed, peers)
    place1, target2, place2, target3 = call(
        functools.partial(route_kernel, size, capacity), "route", (places, index, places, index)
    )(tags)

    for layer, place, target in ((0, place1, target2), (1, place2, target3)):
        packed = run_block(
            layer, place, target, received, attention_gain, attention_in,
            attention_out, feedforward_gain, feedforward_up, feedforward_down,
        )
        received = exchange(packed, peers)

    return pl.pallas_call(
        unpack_kernel,
        name="unpack",
        out_shape=shape(size, width, bf16),
        in_specs=[vmem] + [hbm] * count,
        out_specs=vmem,
        scratch_shapes=[
            pltpu.VMEM((slots, width), bf16),
            pltpu.VMEM((size, 128), i32),
            pltpu.SemaphoreType.DMA((count,)),
        ],
        compiler_params=pltpu.CompilerParams(vmem_limit_bytes=32 << 20),
        cost_estimate=pl.CostEstimate(flops=select, bytes_accessed=0, transcendentals=0),
    )(source3, *received)


def solution(mesh):
    split = P(AXES, None)
    return jax.shard_map(
        body,
        mesh=mesh,
        in_specs=(split, P(AXES), P(AXES), P(), P(), P(), P(), P(), P()),
        out_specs=split,
        check_vma=False,
    )
```

```python
import functools

import jax
import jax.numpy as jnp
from jax import lax
from jax.experimental import pallas as pl
from jax.experimental.pallas import tpu as pltpu
from jax.sharding import PartitionSpec as P

HEADS = 32
PATCH = 1024
EPSILON = 1e-05
LOG2E = 1.4426950408889634
AXES = ("gx", "gy")
SAFE_EXPONENT = 80.0

bf16 = jnp.bfloat16
f32 = jnp.float32
i32 = jnp.int32


def call(kernel, name, out_shape, scratch=(), flops=0):
    def run(*args):
        vmem = pl.BlockSpec(memory_space=pltpu.VMEM)
        outs = jax.tree.map(lambda _: vmem, out_shape)
        moved = sum(a.size * a.dtype.itemsize for a in args)
        return pl.pallas_call(
            kernel,
            name=name,
            out_shape=out_shape,
            in_specs=[vmem] * len(args),
            out_specs=outs,
            scratch_shapes=scratch,
            compiler_params=pltpu.CompilerParams(vmem_limit_bytes=56 << 20),
            cost_estimate=pl.CostEstimate(flops=flops, bytes_accessed=moved, transcendentals=0),
        )(*args)

    return run


def column(row):
    return jnp.broadcast_to(row, (128, row.shape[1])).T


def order_in_bucket(keys, size):
    shift = size.bit_length() - 1
    tall = column(keys)
    pieces = []
    for start in range(0, keys.shape[1], 128):
        piece = keys[:, start : start + 128]
        low = lax.shift_left(lax.shift_right_logical(piece, shift), shift)
        inside = jnp.logical_and(tall >= low, tall < piece)
        pieces.append(jnp.sum(jnp.where(inside, 1.0, 0.0), axis=0, keepdims=True))
    return jnp.concatenate(pieces, axis=1).astype(i32)


def digits(*values):
    rows = []
    for value, count in values:
        for place in range(count):
            rows.append(
                jnp.bitwise_and(lax.shift_right_logical(value, 8 * place), 255).astype(f32)
            )
    rows += [jnp.zeros_like(rows[0])] * (8 - len(rows))
    return jnp.concatenate(rows, axis=0).astype(bf16)


def undigits(rows, start, count):
    value = rows[start : start + 1].astype(i32)
    for place in range(1, count):
        value = value + lax.shift_left(rows[start + place : start + place + 1].astype(i32), 8 * place)
    return value


def chosen(wanted, axis, start, rows, columns):
    index = lax.broadcasted_iota(i32, (rows, columns), axis) + start
    return jnp.where(wanted == index, 1.0, 0.0).astype(bf16)


def contract_last(a, b):
    return lax.dot_general(a, b, (((1,), (1,)), ((), ())), preferred_element_type=f32)


def my_index():
    return lax.axis_index("gx") * lax.axis_size("gy") + lax.axis_index("gy")


def send_tags_kernel(size, capacity, zr_ref, hr_ref, tag_ref, target_ref, source_ref):
    shift = size.bit_length() - 1
    peers = tag_ref.shape[0]
    zr, hr = zr_ref[...], hr_ref[...]
    row = lax.broadcasted_iota(i32, (1, size), 1)
    z_owner = lax.shift_right_logical(zr, shift)
    h_owner = lax.shift_right_logical(hr, shift)
    z_place = order_in_bucket(z_owner * size + row, size)
    h_place = order_in_bucket(hr, size)
    me = my_index()
    target_ref[...] = jnp.bitwise_xor(z_owner, me) * capacity + z_place
    source_ref[...] = jnp.bitwise_xor(h_owner, me) * capacity + h_place
    ones = jnp.ones_like(zr)
    peer = lax.broadcasted_iota(i32, (peers, 1), 0)
    lane = lax.broadcasted_iota(i32, (128, 1), 0)
    for i, (owner, place, near, far) in enumerate(
        ((z_owner, z_place, zr, hr), (h_owner, h_place, hr, zr))
    ):
        parts = digits((jnp.bitwise_and(near, size - 1), 2), (far, 3), (ones, 1)).astype(f32)
        mine = jnp.where(owner == peer, 1.0, 0.0)
        spread = jnp.where(place == lane, 1.0, 0.0).astype(bf16)
        tall = jnp.concatenate([mine * parts[d : d + 1] for d in range(6)], axis=0).astype(bf16)
        found = contract_last(tall, spread).astype(i32)

        def value(first, count):
            total = found[first * peers : (first + 1) * peers]
            for d in range(1, count):
                low = (first + d) * peers
                total = total + lax.shift_left(found[low : low + peers], 8 * d)
            return total

        tag_ref[:, i * 128 : (i + 1) * 128] = jnp.where(
            value(5, 1) > 0, value(2, 3) * size + value(0, 2), -1
        )


def from_xor(table, me):
    peers = table.shape[0]
    row = lax.broadcasted_iota(i32, table.shape, 0)
    bit = 1
    while bit < peers:
        up = pltpu.roll(table, peers - bit, 0)
        down = pltpu.roll(table, bit, 0)
        swapped = jnp.where(jnp.bitwise_and(row, bit) == 0, up, down)
        table = jnp.where(jnp.bitwise_and(me, bit) == 0, table, swapped)
        bit *= 2
    return table


def offsets(counts):
    peers = counts.shape[0]
    row = lax.broadcasted_iota(i32, counts.shape, 0)
    total = counts
    step = 1
    while step < peers:
        total = total + jnp.where(row >= step, pltpu.roll(total, step, 0), 0)
        step *= 2
    return total - counts


def positions_of_slots(counts, first, capacity, begin, ref):
    peers = counts.shape[0]
    owner = lax.broadcasted_iota(i32, (peers, 128), 0)
    for start in range(0, ref.shape[1], 128):
        slot = lax.broadcasted_iota(i32, (peers, 128), 1) + (begin + start)
        place = slot - owner * capacity
        mine = jnp.logical_and(place >= 0, place < counts)
        ref[:, start : start + 128] = (
            jnp.sum(jnp.where(mine, first + place + 1, 0), axis=0, keepdims=True) - 1
        )


def listed(tags, size):
    peers = tags.shape[0]
    counts = jnp.sum(jnp.where(tags >= 0, 1.0, 0.0), axis=1, keepdims=True).astype(i32)
    counts = jnp.broadcast_to(counts, (peers, 128))
    first = offsets(counts)
    position = lax.broadcasted_iota(i32, (1, size), 1)
    wide_first = jnp.concatenate([first] * (size // 128), axis=1)
    wide_end = jnp.concatenate([first + counts] * (size // 128), axis=1)
    within = jnp.logical_and(position >= wide_first, position < wide_end)
    mine = jnp.where(within, 1.0, 0.0)
    owner_index = lax.broadcasted_iota(i32, (peers, size), 0)
    owner = jnp.sum(jnp.where(within, owner_index, 0), axis=0, keepdims=True)
    place = position - jnp.sum(jnp.where(within, wide_first, 0), axis=0, keepdims=True)
    at_place = lax.broadcasted_iota(i32, (128, size), 0) == place
    shift = size.bit_length() - 1
    clean = jnp.maximum(tags, 0)
    near, far = jnp.bitwise_and(clean, size - 1), lax.shift_right_logical(clean, shift)
    mine = mine.astype(bf16)

    def fetch(values, count):
        total = jnp.zeros((1, size), i32)
        for d in range(count):
            digit = jnp.bitwise_and(lax.shift_right_logical(values, 8 * d), 255)
            spread = lax.dot_general(
                digit.astype(f32).astype(bf16), mine, (((0,), (0,)), ((), ())),
                preferred_element_type=f32,
            )
            picked = jnp.sum(jnp.where(at_place, spread, 0.0), axis=0, keepdims=True)
            total = total + lax.shift_left(picked.astype(i32), 8 * d)
        return total

    return owner, fetch(near, 2), fetch(far, 3), counts, first


def route_kernel(size, capacity, late, tag_ref, *refs):
    early1_ref, late1_ref, target2_ref, early2_ref, late2_ref, target3_ref = refs
    shift = size.bit_length() - 1
    peers = tag_ref.shape[0]
    begin = (peers - late) * capacity
    me = my_index()
    tags = from_xor(tag_ref[...], me)
    owner, zs, hr, counts, first = listed(tags[:, :128], size)
    limited = jnp.where(lax.broadcasted_iota(i32, counts.shape, 0) < peers - late, counts, 0)
    positions_of_slots(limited, first, capacity, 0, early1_ref)
    positions_of_slots(counts, first, capacity, begin, late1_ref)
    goal = jnp.bitwise_xor(lax.shift_right_logical(hr, shift), me)
    target2_ref[...] = goal * capacity + order_in_bucket(goal * size + zs, size)
    home, hs, zr, counts, first = listed(tags[:, 128:], size)
    key = jnp.bitwise_xor(zr, me * size)
    position = order_in_bucket(key, size * peers)
    came = lax.shift_right_logical(key, shift)
    came_from = came == lax.broadcasted_iota(i32, (peers, size), 0)
    counts = jnp.sum(jnp.where(came_from, 1.0, 0.0), axis=1, keepdims=True).astype(i32)
    counts = jnp.broadcast_to(counts, (peers, 128))
    first = offsets(counts)
    limited = jnp.where(lax.broadcasted_iota(i32, counts.shape, 0) < peers - late, counts, 0)
    positions_of_slots(limited, first, capacity, 0, early2_ref)
    positions_of_slots(counts, first, capacity, begin, late2_ref)
    target = home * capacity + order_in_bucket(home * size + hs, size)
    parts = digits((target, 2))
    for start in range(0, size, 256):
        picked = contract_last(parts, chosen(position, 0, start, 256, size))
        target3_ref[:, start : start + 256] = undigits(picked, 0, 2)


def issue_order(count):
    if count == 1:
        return [0]
    half = count // 2
    order = []
    for i in range(half):
        order += [half + i, i + 1]
    return [part % half if part == half and i else part for i, part in enumerate(order[:-1])] + [0]


def pack_rows(target_ref, rows_ref, packed_ref, listed_refs, sem):
    slots = packed_ref.shape[0]
    count = len(listed_refs)
    capacity = slots // count
    part_refs = [None] * count
    for ref, part in zip(listed_refs, issue_order(count)):
        part_refs[part] = ref

    def step(i, carry):
        start = pl.multiple_of(i * 256, 256)
        pick = chosen(target_ref[...], 0, start, 256, rows_ref.shape[0])
        packed_ref[pl.ds(start, 256), :] = jnp.dot(
            pick, rows_ref[...], preferred_element_type=f32
        ).astype(bf16)
        return carry

    copies = []
    blocks = slots // 256
    for done in range(0, blocks, 4):
        end = min(done + 4, blocks)
        lax.fori_loop(done, end, step, 0)
        while (len(copies) + 1) * capacity <= end * 256 and len(copies) < count:
            i = len(copies)
            copies.append(
                pltpu.make_async_copy(
                    packed_ref.at[pl.ds(i * capacity, capacity)], part_refs[i], sem.at[i]
                )
            )
            copies[-1].start()
    for copy in copies:
        copy.wait()


def pack_kernel(target_ref, rows_ref, *rest):
    *part_refs, packed_ref, sem = rest
    pack_rows(target_ref, rows_ref, packed_ref, part_refs, sem)


def load_parts(part_refs, received_ref, sem):
    copies = []
    start = 0
    for i, part in enumerate(part_refs):
        rows = part.shape[0]
        copies.append(
            pltpu.make_async_copy(part, received_ref.at[pl.ds(start, rows)], sem.at[i])
        )
        copies[-1].start()
        start += rows
    if start < received_ref.shape[0]:
        received_ref[start:, :] = jnp.zeros((received_ref.shape[0] - start, part.shape[1]), bf16)
    return copies


def unpack_kernel(begin, last, source_ref, *rest):
    if last:
        before_ref, *rest = rest
    *part_refs, out_ref, received_ref, tall_ref, sem = rest
    copies = load_parts(part_refs, received_ref, sem)
    slots = received_ref.shape[0]
    tall_ref[...] = column(source_ref[...])
    for copy in copies:
        copy.wait()

    def step(i, carry):
        start = pl.multiple_of(i * 256, 256)
        tall = tall_ref[pl.ds(start, 256), :]
        pick = jnp.concatenate(
            [chosen(tall, 1, begin + piece, 256, 128) for piece in range(0, slots, 128)], axis=1
        )
        rows = jnp.dot(pick, received_ref[...], preferred_element_type=f32)
        if last:
            rows = rows + before_ref[pl.ds(start, 256), :].astype(f32)
        out_ref[pl.ds(start, 256), :] = rows.astype(bf16)
        return carry

    lax.fori_loop(0, out_ref.shape[0] // 256, step, 0)


def normalize(values, gain):
    values = values.astype(f32)
    centred = values - jnp.mean(values, axis=-1, keepdims=True)
    variance = jnp.mean(centred * centred, axis=-1, keepdims=True)
    return (centred * lax.rsqrt(variance + EPSILON) * gain).astype(bf16)


def head_operands(head, heads, q_ref):
    head_size = q_ref.shape[1] // heads
    per_group = 128 // head_size
    lane_head = lax.broadcasted_iota(i32, (1, 128), 1) // head_size
    group = pl.multiple_of((head // per_group) * 128, 128)
    return group, pl.multiple_of(head * head_size, head_size), lane_head == head % per_group


def weighted(keys, queries, values, ones):
    weights = jnp.exp2(contract_last(keys, queries)).astype(bf16)
    return jnp.dot(jnp.concatenate([values, ones], axis=0), weights, preferred_element_type=f32)


def attend_early(heads, q_ref, k_ref, vt_ref, partial_ref):
    size, width = q_ref.shape
    head_size = width // heads
    keep = partial_ref.shape[0] // heads
    ones = jnp.ones((16, size), bf16)
    together = 2

    def step(i, carry):
        for part in range(together):
            head = i * together + part
            group, first, mine = head_operands(head, heads, q_ref)
            keys = jnp.where(mine, k_ref[:, pl.ds(group, 128)], jnp.zeros((), bf16))
            mixed = weighted(
                keys, q_ref[:, pl.ds(group, 128)], vt_ref[pl.ds(first, head_size), :], ones
            )
            partial_ref[pl.ds(pl.multiple_of(head * keep, keep), keep), :] = mixed[:keep]
        return carry

    lax.fori_loop(0, heads // together, step, 0)


def attend_late(heads, split, small, q_ref, k_ref, vt_ref, partial_ref, out_ref):
    size, width = q_ref.shape
    head_size = width // heads
    keep = partial_ref.shape[0] // heads
    none = jnp.zeros((), bf16)
    ones = jnp.ones((16, size), bf16)

    def finish(first, start, count, mixed):
        out_ref[pl.ds(first, head_size), pl.ds(start, count)] = (
            mixed[:head_size] / mixed[head_size : head_size + 1]
        ).astype(bf16)

    together = 2

    def small_scores(i, carry):
        for part in range(together):
            head = i * together + part
            group, first, mine = head_operands(head, heads, q_ref)
            keys = jnp.where(mine, k_ref[:, pl.ds(group, 128)], none)
            queries = q_ref[:, pl.ds(group, 128)]
            values = vt_ref[pl.ds(first, head_size), :]
            late = weighted(keys[split:], queries, values[:, split:], ones[:, split:])
            cross = weighted(keys[:split], queries[split:], values[:, :split], ones[:, :split])
            before = partial_ref[pl.ds(pl.multiple_of(head * keep, keep), keep), :]
            finish(first, 0, split, late[:keep, :split] + before)
            finish(first, split, size - split, late[:keep, split:] + cross[:keep])
        return carry

    def any_scores(head, carry):
        group, first, mine = head_operands(head, heads, q_ref)
        keys = jnp.where(mine, k_ref[:, pl.ds(group, 128)], none)
        values = jnp.concatenate([vt_ref[pl.ds(first, head_size), :], ones], axis=0)

        def tile(t, inner):
            start = pl.multiple_of(t * 256, 256)
            scores = contract_last(keys, q_ref[pl.ds(start, 256), pl.ds(group, 128)])
            scores = scores - jnp.max(scores, axis=0, keepdims=True)
            weights = jnp.exp2(scores).astype(bf16)
            finish(first, start, 256, jnp.dot(values, weights, preferred_element_type=f32))
            return inner

        return lax.fori_loop(0, size // 256, tile, carry)

    @pl.when(small)
    def _():
        lax.fori_loop(0, heads // together, small_scores, 0)

    @pl.when(jnp.logical_not(small))
    def _():
        lax.fori_loop(0, heads, any_scores, 0)


def gelu(x):
    return (0.5 * x) * (1.0 + lax.erf(x * 0.7071067811865476))


def project(rows, start, heads, gain_ref, in_ref, q_ref, k_ref, vt_ref, most):
    block, width = rows.shape
    head_size = width // heads
    group = jnp.where(
        lax.broadcasted_iota(i32, (width, 128), 0) // head_size
        == lax.broadcasted_iota(i32, (width, 128), 1),
        1.0,
        0.0,
    ).astype(bf16)
    normed = normalize(rows, gain_ref[...])
    q = jnp.dot(normed, in_ref[:, :width], preferred_element_type=f32)
    q = (q * (head_size ** (-0.5) * LOG2E)).astype(bf16)
    k = jnp.dot(normed, in_ref[:, width : 2 * width], preferred_element_type=f32).astype(bf16)
    v = jnp.dot(normed, in_ref[:, 2 * width :], preferred_element_type=f32)
    q_ref[pl.ds(start, block), :] = q
    k_ref[pl.ds(start, block), :] = k
    vt_ref[:, pl.ds(start, block)] = v.T.astype(bf16)
    sizes = [jnp.dot(x * x, group, preferred_element_type=f32) for x in (q, k)]
    return [jnp.maximum(m, jnp.max(x, axis=0, keepdims=True)) for m, x in zip(most, sizes)]


def small_enough(most):
    return jnp.max(most[0] * most[1]) <= SAFE_EXPONENT * SAFE_EXPONENT


def early_kernel(layer, heads, place_ref, gain_ref, in_hbm, *refs):
    *part_refs, rows_ref, q_ref, k_ref, vt_ref, partial_ref, most_ref = refs[:-4]
    received_ref, in_ref, load_sem, part_sem = refs[-4:]
    arrivals = load_parts(part_refs, received_ref, part_sem)
    load = pltpu.make_async_copy(in_hbm.at[layer], in_ref, load_sem.at[0])
    load.start()
    block = 256
    split = q_ref.shape[0]
    for arrival in arrivals:
        arrival.wait()
    load.wait()

    def unpack(start):
        pick = chosen(place_ref[...], 0, start, block, received_ref.shape[0])
        rows = jnp.dot(pick, received_ref[...], preferred_element_type=f32).astype(bf16)
        rows_ref[pl.ds(start, block), :] = rows
        return rows

    def front(i, most):
        start = pl.multiple_of(i * block, block)
        rows = unpack(start)
        return project(rows, start, heads, gain_ref, in_ref, q_ref, k_ref, vt_ref, most)

    zero = jnp.zeros((1, 128), f32)
    most = lax.fori_loop(0, split // block, front, [zero, zero])
    most_ref[0:1, :], most_ref[1:2, :] = most

    @pl.when(small_enough(most))
    def _():
        attend_early(heads, q_ref, k_ref, vt_ref, partial_ref)

    def back(i, carry):
        unpack(pl.multiple_of(i * block, block))
        return carry

    lax.fori_loop(split // block, rows_ref.shape[0] // block, back, 0)


def late_kernel(layer, heads, late, *refs):
    place_ref, target_ref, gain_in_ref, gain_feed_ref, most_ref = refs[:5]
    in_hbm, out_hbm, up_hbm, down_hbm, rows_hbm, q_hbm, k_hbm, vt_hbm, partial_hbm = refs[5:14]
    late_refs = refs[14 : 14 + late]
    (
        received_ref, in_ref, out_ref, up_ref, down_ref, packed_ref, rows_ref, q_ref, k_ref,
        vt_ref, partial_ref, mixed_ref, block_ref, load_sem, part_sem, store_sem,
    ) = refs[-16:]
    packed_refs = refs[14 + late : -16]
    size, width = rows_ref.shape
    hidden = up_ref.shape[1]
    split = partial_ref.shape[1]
    arrivals = load_parts(late_refs, received_ref, part_sem) if late else []
    loads = [
        pltpu.make_async_copy(source, target, load_sem.at[i])
        for i, (source, target) in enumerate(
            (
                (rows_hbm, rows_ref),
                (in_hbm.at[layer], in_ref),
                (q_hbm, q_ref.at[pl.ds(0, split)]),
                (k_hbm, k_ref.at[pl.ds(0, split)]),
                (vt_hbm, vt_ref.at[:, pl.ds(0, split)]),
                (partial_hbm, partial_ref),
                (out_hbm.at[layer], out_ref),
                (up_hbm.at[layer], up_ref),
                (down_hbm.at[layer], down_ref),
            )
        )
    ]
    for load in loads:
        load.start()
    block = 256
    for arrival in arrivals:
        arrival.wait()
    for load in loads[:2]:
        load.wait()

    def back(i, most):
        start = pl.multiple_of(i * block, block)
        rows = rows_ref[pl.ds(start, block), :]
        if late:
            pick = chosen(place_ref[...], 0, start, block, received_ref.shape[0])
            came = jnp.dot(pick, received_ref[...], preferred_element_type=f32)
            rows = (rows.astype(f32) + came).astype(bf16)
            rows_ref[pl.ds(start, block), :] = rows
        return project(rows, start, heads, gain_in_ref, in_ref, q_ref, k_ref, vt_ref, most)

    most = lax.fori_loop(
        split // block, size // block, back, [most_ref[0:1, :], most_ref[1:2, :]]
    )
    for load in loads[2:6]:
        load.wait()
    attend_late(heads, split, small_enough(most), q_ref, k_ref, vt_ref, partial_ref, mixed_ref)
    for load in loads[6:]:
        load.wait()
    piece = 512

    def feed(i, carry):
        start = pl.multiple_of(i * block, block)
        mixed = lax.dot_general(
            mixed_ref[:, pl.ds(start, block)],
            out_ref[...],
            (((0,), (0,)), ((), ())),
            preferred_element_type=f32,
        )
        stream = (rows_ref[pl.ds(start, block), :].astype(f32) + mixed).astype(bf16)
        normed = normalize(stream, gain_feed_ref[...])
        total = stream.astype(f32)
        for first in range(0, hidden, piece):
            up = jnp.dot(normed, up_ref[:, first : first + piece], preferred_element_type=f32)
            total = total + jnp.dot(
                gelu(up).astype(bf16), down_ref[first : first + piece, :], preferred_element_type=f32
            )
        block_ref[pl.ds(start, block), :] = total.astype(bf16)
        return carry

    lax.fori_loop(0, size // block, feed, 0, unroll=2)
    pack_rows(target_ref, block_ref, packed_ref, packed_refs, store_sem)


VMEM = pl.BlockSpec(memory_space=pltpu.VMEM)
HBM = pl.BlockSpec(memory_space=pl.ANY)


def parts_shape(slots, count, width):
    return [jax.ShapeDtypeStruct((slots // count, width), bf16)] * count


def params(mib):
    return pltpu.CompilerParams(vmem_limit_bytes=mib << 20)


def cost(flops, moved):
    return pl.CostEstimate(flops=flops, bytes_accessed=moved, transcendentals=0)


def run_block(
    layer, late, early_place, late_place, target, parts,
    gains_in, w_in, w_out, gains_feed, up, down,
):
    count = len(parts)
    width = parts[0].shape[1]
    slots = count * parts[0].shape[0]
    size = target.shape[1]
    hidden = up.shape[2]
    split = size // 2
    early_slots, late_slots = early_place.shape[1], late_place.shape[1]
    keep = width // HEADS + 8
    gain_in = gains_in[layer].reshape(1, width)
    shape = jax.ShapeDtypeStruct
    rows, q, k, vt, partial, most = pl.pallas_call(
        functools.partial(early_kernel, layer, HEADS),
        name="early",
        out_shape=(
            shape((size, width), bf16),
            shape((split, width), bf16),
            shape((split, width), bf16),
            shape((width, split), bf16),
            shape((HEADS * keep, split), f32),
            shape((2, 128), f32),
        ),
        in_specs=[VMEM, VMEM, HBM] + [HBM] * (count - late),
        out_specs=[VMEM] * 6,
        scratch_shapes=[
            pltpu.VMEM((early_slots, width), bf16),
            pltpu.VMEM((width, 3 * width), bf16),
            pltpu.SemaphoreType.DMA((1,)),
            pltpu.SemaphoreType.DMA((count - late,)),
        ],
        compiler_params=params(40),
        cost_estimate=cost(
            2 * early_slots * size * width + 6 * split * width * width + 16 * split * split * width,
            2 * early_slots * width,
        ),
    )(early_place, gain_in, w_in, *parts[: count - late])
    half = pltpu.VMEM((size, width), bf16)
    flipped = pltpu.VMEM((width, size), bf16)
    return pl.pallas_call(
        functools.partial(late_kernel, layer, HEADS, late),
        name="late",
        out_shape=parts_shape(slots, count, width),
        in_specs=[VMEM] * 5 + [HBM] * (9 + late),
        out_specs=[HBM] * count,
        scratch_shapes=[
            pltpu.VMEM((late_slots, width), bf16),
            pltpu.VMEM((width, 3 * width), bf16),
            pltpu.VMEM((width, width), bf16),
            pltpu.VMEM((width, hidden), bf16),
            pltpu.VMEM((hidden, width), bf16),
            pltpu.VMEM((slots, width), bf16),
            half,
            half,
            half,
            flipped,
            pltpu.VMEM((HEADS * keep, split), f32),
            flipped,
            half,
            pltpu.SemaphoreType.DMA((9,)),
            pltpu.SemaphoreType.DMA((max(late, 1),)),
            pltpu.SemaphoreType.DMA((count,)),
        ],
        compiler_params=params(48),
        cost_estimate=cost(
            2 * slots * size * width + size * width * (8 * width + 4 * hidden + 12 * size),
            4 * slots * width,
        ),
    )(
        late_place, target, gain_in, gains_feed[layer].reshape(1, width), most,
        w_in, w_out, up, down, rows, q, k, vt, partial, *parts[count - late :],
    )


def exchange(listed_parts, peers):
    count = len(listed_parts)
    if count == peers:
        out = [None] * peers
        for s, part in zip(issue_order(count), listed_parts):
            out[s] = lax.ppermute(part, AXES, [(d, d ^ s) for d in range(peers)]) if s else part
        return out
    (part,) = listed_parts
    turn = jnp.bitwise_xor(jnp.arange(peers, dtype=i32), my_index())
    stacked = part.reshape(peers, part.shape[0] // peers, part.shape[1])
    stacked = jnp.take(stacked, turn, axis=0)
    received = lax.all_to_all(stacked, AXES, split_axis=0, concat_axis=0, tiled=True)
    return [jnp.take(received, turn, axis=0).reshape(part.shape)]


def body(
    features, zorder_rank, hilbert_rank, attention_gain, attention_in, attention_out,
    feedforward_gain, feedforward_up, feedforward_down,
):
    size, width = features.shape
    peers = lax.axis_size("gx") * lax.axis_size("gy")
    capacity = 5 * size // (2 * peers)
    slots = peers * capacity
    count = peers if peers <= 64 and capacity % 16 == 0 else 1

    def shape(rows, columns, dtype):
        return jax.ShapeDtypeStruct((rows, columns), dtype)

    index = shape(1, size, i32)
    late = count // 8
    late_slots = late * capacity
    early_slots = slots - late_slots
    early_places = shape(1, pl.cdiv(early_slots, 256) * 256, i32)
    late_places = shape(1, max(pl.cdiv(late_slots, 128) * 128, 128), i32)
    tags, target1, source3 = call(
        functools.partial(send_tags_kernel, size, capacity),
        "send_tags",
        (shape(peers, 256, i32), index, index),
    )(zorder_rank.reshape(1, size), hilbert_rank.reshape(1, size))
    tags = lax.all_to_all(
        tags.reshape(peers, 1, 256), AXES, split_axis=0, concat_axis=0, tiled=True
    ).reshape(peers, 256)
    tags, target1 = lax.optimization_barrier((tags, target1))
    packed = pl.pallas_call(
        pack_kernel,
        name="pack",
        out_shape=parts_shape(slots, count, width),
        in_specs=[VMEM, VMEM],
        out_specs=[HBM] * count,
        scratch_shapes=[pltpu.VMEM((slots, width), bf16), pltpu.SemaphoreType.DMA((count,))],
        compiler_params=params(32),
        cost_estimate=cost(2 * slots * size * width, 2 * slots * width),
    )(target1, features)
    received = exchange(packed, peers)
    early1, late1, target2, early2, late2, target3 = call(
        functools.partial(route_kernel, size, capacity, late * (peers // count)),
        "route",
        (early_places, late_places, index, early_places, late_places, index),
    )(tags)

    for layer, places, target in ((0, (early1, late1), target2), (1, (early2, late2), target3)):
        packed = run_block(
            layer, late, *places, target, received, attention_gain, attention_in,
            attention_out, feedforward_gain, feedforward_up, feedforward_down,
        )
        received = exchange(packed, peers)

    def unpack(begin, last, places, before, parts):
        return pl.pallas_call(
            functools.partial(unpack_kernel, begin, last),
            name="unpack_late" if last else "unpack",
            out_shape=shape(size, width, bf16),
            in_specs=[VMEM] * (1 + len(before)) + [HBM] * len(parts),
            out_specs=VMEM,
            scratch_shapes=[
                pltpu.VMEM((places.shape[1], width), bf16),
                pltpu.VMEM((size, 128), i32),
                pltpu.SemaphoreType.DMA((len(parts),)),
            ],
            compiler_params=params(32),
            cost_estimate=cost(2 * places.shape[1] * size * width, 2 * slots * width),
        )(source3, *before, *parts)

    rows = unpack(0, False, early_places, [], received[: count - late])
    if late:
        rows = unpack(early_slots, True, late_places, [rows], received[count - late :])
    return rows


def solution(mesh):
    split = P(AXES, None)
    return jax.shard_map(
        body,
        mesh=mesh,
        in_specs=(split, P(AXES), P(AXES), P(), P(), P(), P(), P(), P()),
        out_specs=split,
        check_vma=False,
    )
```
